32 devices in a mesh: groups: 2 (over x), gx: 16 (over z, y, core).
Axes of the slice: x: 2, y: 2, z: 4, core: 2. Of those that a mesh axis runs over, the one named last changes fastest.
Arguments:
- wave_one: float32 [2, 512, 2048], P(None, 'groups', 'gx'), parts along dimension 1, may hold values from -6 to 6
- wave_two: float32 [2, 512, 2048], P(None, 'groups', 'gx'), parts along dimension 1, may hold values from -4.2 to 4.2
- mismatch: float32 [512, 2048], P('groups', 'gx'), parts along dimension 0, may hold values from -1.2 to 1.2
- plate: int32 [16, 64], P('groups', 'gx'), parts along dimension 0, may hold values from 0 to 15
- spot_low: int32 [1024], P('groups'), parts along dimension 0, may hold values from 64 to 255
- spot_high: int32 [1024], P('groups'), parts along dimension 0, may hold values from 256 to 447
- row_gain: float32 [1024], P('groups'), parts along dimension 0, may hold values from 0.5 to 3
- column_gain: float32 [1024], P('groups'), parts along dimension 0, may hold values from 0.5 to 3
Outputs:
- third: float32 [2, 512, 2048], P(None, 'groups', 'gx'), parts along dimension 1
- far_field: float32 [2, 1024, 512], P(None, ('groups', 'gx')), parts along dimension 1
- back_field: float32 [2, 512, 2048], P(None, 'groups', 'gx'), parts along dimension 1
The draws below stay inside these ranges and needn't reach their ends.
There are 2 independent parts, one for each index of `groups`. The reference program is written for one: setup_inputs(seed, part) draws one part's arguments, and reference() takes and returns one part's arrays. A program takes and returns all parts, laid end to end along the dimension named above; each array names one. Nothing has to cross between parts.
All inputs are finite; a program needn't handle non-finite values.
Results may differ from the reference program's by a relative error of at most 0.00017.
Values sent between devices are 32-bit elements; how exact they have to be, the bound alone decides.
A program may use at most 64 MiB of HBM per device.

```python
import math
import jax
import jax.numpy as jnp
from jax import lax

NY = 256
FFY = 512
FFX = 512
SUBSTEPS = 4
ZOOM = 4
LEVELS = 16
PLATE = 32
NX = 2048
PY = 8
PX = 64


def set_ends(drawn, key, low, high):
    longest = drawn.shape.index(max(drawn.shape))
    spots = []
    for shift in (0, 1):
        where = [jax.random.randint(jax.random.fold_in(key, axis), (), 0, length) for axis, length in enumerate(drawn.shape)]
        where[longest] = (where[longest] + shift) % drawn.shape[longest]
        spots.append(tuple(where))
    return drawn.at[spots[0]].set(low).at[spots[1]].set(high)


def block_scale(stream_key, dims, shards, least, top_value):
    def one(axis_at, shards_of):
        draws = jax.random.uniform(jax.random.fold_in(jax.random.fold_in(stream_key, 6), axis_at), (shards_of,), jnp.float32, least / len(shards), top_value / len(shards))
        return jnp.repeat(jnp.exp(draws), dims[axis_at] // shards_of).reshape((-1,) + (1,) * (len(dims) - axis_at - 1))

    level = one(*shards[0])
    for cut in shards[1:]:
        level = level * one(*cut)
    return level


def scatter_about(key, shape, scale, reach, pieces=(), held_as=jnp.bfloat16):
    array = jax.random.normal(key, shape, jnp.float32) * scale
    if len(pieces) > 0:
        array = block_scale(key, shape, pieces, -0.22, 0.18) * array
    return jnp.clip(array, min=-reach, max=reach).astype(held_as)


def setup_inputs(seed: int = 0, part: int = 0) -> dict:
    splits = jax.random.split(jax.random.key(seed), 9)
    part_splits = jax.random.split(jax.random.fold_in(splits[8], part), 9)
    wave_one = scatter_about(part_splits[0], (2, NY, NX), 1.0, 6.0, ((2, 16),), jnp.float32)
    wave_two = scatter_about(part_splits[1], (2, NY, NX), 0.7, 4.2, ((2, 16),), jnp.float32)
    mismatch = jnp.clip(jax.random.uniform(part_splits[2], (NY, NX), jnp.float32, -1.2, 1.2) * block_scale(part_splits[2], (NY, NX), ((1, 16),), -0.4, 0.0), -1.2, 1.2)
    plate = set_ends(jax.random.randint(part_splits[3], (PY, PX), 0, LEVELS), jax.random.fold_in(part_splits[3], 1), 0, LEVELS - 1).astype(jnp.int32)
    spot_low = set_ends(jax.random.randint(part_splits[4], (FFY,), FFX // 8, FFX // 2), jax.random.fold_in(part_splits[4], 1), FFX // 8, (FFX // 2) - 1).astype(jnp.int32)
    spot_high = set_ends(jax.random.randint(part_splits[5], (FFY,), FFX // 2, 7 * FFX // 8), jax.random.fold_in(part_splits[5], 1), FFX // 2, (7 * FFX // 8) - 1).astype(jnp.int32)
    row_gain = jnp.clip(jnp.exp(jax.random.uniform(part_splits[6], (FFY,), jnp.float32, math.log(0.5), math.log(3.0))), 0.5, 3.0)
    column_gain = jnp.clip(jnp.exp(jax.random.uniform(part_splits[7], (FFX,), jnp.float32, math.log(0.5), math.log(3.0))), 0.5, 3.0)
    return dict(wave_one=wave_one, wave_two=wave_two, mismatch=mismatch, plate=plate, spot_low=spot_low, spot_high=spot_high, row_gain=row_gain, column_gain=column_gain)


DIFFRACT = (0.08, 0.04, 0.027)
WALKOFF = (0.3, -0.8, 0.8)
COUPLE = (0.08, 0.16, 0.24)
FAR_SCALE = 4.0
PRECISE = lax.Precision.HIGHEST

def complex_mul(first_real, first_imaginary, second_real, second_imaginary):
    return (first_real * second_real - first_imaginary * second_imaginary, first_real * second_imaginary + first_imaginary * second_real)

def complex_dot(left_pair, right_pair, contract):

    def product(first, second):
        return lax.dot_general(first, second, (contract, ((), ())), precision=PRECISE, preferred_element_type=jnp.float32)
    real = product(left_pair[0], right_pair[0]) - product(left_pair[1], right_pair[1])
    imaginary = product(left_pair[0], right_pair[1]) + product(left_pair[1], right_pair[0])
    return (real, imaginary)

def increments(fields, mismatch_mid, position):
    middle = fields[:, :, 1:-1]
    left = fields[:, :, :-2]
    right = fields[:, :, 2:]
    blank = jnp.zeros_like(middle[:, :1])
    above = jnp.concatenate([blank, middle[:, :-1]], axis=1)
    below = jnp.concatenate([middle[:, 1:], blank], axis=1)
    laplace = above + below + left + right - 4.0 * middle
    phase = mismatch_mid * position
    cosine = jnp.cos(phase)
    sine_part = jnp.sin(phase)
    term = complex_mul(middle[4], middle[5], middle[2], -middle[3])
    mix_one = complex_mul(term[0], term[1], cosine, -sine_part)
    term = complex_mul(middle[4], middle[5], middle[0], -middle[1])
    mix_two = complex_mul(term[0], term[1], cosine, -sine_part)
    term = complex_mul(middle[0], middle[1], middle[2], middle[3])
    mix_three = complex_mul(term[0], term[1], cosine, sine_part)
    mixing = (mix_one, mix_two, mix_three)
    rates = []
    for wave in range(3):
        spread = DIFFRACT[wave]
        drift = WALKOFF[wave]
        strength = COUPLE[wave]
        for part in range(2):
            channel = 2 * wave + part
            if drift > 0:
                moving = -drift * (middle[channel] - left[channel])
            else:
                moving = -drift * (right[channel] - middle[channel])
            if part == 0:
                rate = -spread * laplace[channel + 1] - strength * mixing[wave][1]
            else:
                rate = spread * laplace[channel - 1] + strength * mixing[wave][0]
            rates.append(rate + moving)
    return jnp.stack(rates)

def substep(fields, mismatch, position):
    padding = ((0, 0), (0, 0), (1, 1))
    first = increments(jnp.pad(fields, padding), mismatch, position)
    trial = fields + first
    second = increments(jnp.pad(trial, padding), mismatch, position + 1.0)
    return fields + 0.5 * (first + second)

def table(positions, count, period):
    frequency = jnp.arange(count, dtype=jnp.int32) - count // 2
    turns = jnp.mod(frequency[:, None] * positions[None, :], period)
    angle = 2.0 * jnp.pi / period * turns.astype(jnp.float32)
    return (jnp.cos(angle), -jnp.sin(angle))

def replace_amplitude(real, imaginary, position, low, high, gain):
    magnitude = jnp.sqrt(real * real + imaginary * imaginary)
    inside = (position >= low) & (position < high)
    factor = gain / jnp.maximum(magnitude, 1.0)
    return (jnp.where(inside, real * factor, real), jnp.where(inside, imaginary * factor, imaginary))

def reference(wave_one, wave_two, mismatch, plate, spot_low, spot_high, row_gain, column_gain):
    fields = jnp.concatenate([wave_one, wave_two, jnp.zeros_like(wave_one)], axis=0)
    for substep_index in range(SUBSTEPS):
        fields = substep(fields, mismatch, float(substep_index))
    third = fields[4:6]
    levels = jnp.repeat(jnp.repeat(plate, PLATE, axis=0), PLATE, axis=1)
    angle = 2.0 * jnp.pi / LEVELS * levels.astype(jnp.float32)
    cosine = jnp.cos(angle)
    sine_part = jnp.sin(angle)
    near = complex_mul(third[0], third[1], cosine, sine_part)
    scale = FAR_SCALE / math.sqrt(NY * NX)
    row_table = table(jnp.arange(NY, dtype=jnp.int32) - NY // 2, FFY, ZOOM * NY)
    column_table = table(jnp.arange(NX, dtype=jnp.int32) - NX // 2, FFX, FFX)
    rows_done = complex_dot(row_table, near, ((1,), (0,)))
    spectrum = complex_dot(rows_done, column_table, ((1,), (1,)))
    far_real = scale * spectrum[0]
    far_imaginary = scale * spectrum[1]
    position = jnp.arange(FFX, dtype=jnp.int32)[None, :]
    gain = row_gain[:, None] * column_gain[None, :]
    replaced = replace_amplitude(far_real, far_imaginary, position, spot_low[:, None], spot_high[:, None], gain)
    conj_column = (column_table[0], -column_table[1])
    conj_row = (row_table[0], -row_table[1])
    across = complex_dot(replaced, conj_column, ((1,), (0,)))
    summed = complex_dot(conj_row, across, ((0,), (0,)))
    back = complex_mul(scale * summed[0], scale * summed[1], cosine, -sine_part)
    return (third, jnp.stack([far_real, far_imaginary]), jnp.stack([back[0], back[1]]))
```

```python
import math

import jax
import jax.numpy as jnp
import numpy as np
from jax import lax
from jax.experimental import pallas as pl
from jax.experimental.pallas import tpu as pltpu
from jax.sharding import PartitionSpec as P

SUBSTEPS = 4
ZOOM = 4
LEVELS = 16
PLATE = 32

DIFFRACT = (0.08, 0.04, 0.027)
WALKOFF = (0.3, -0.8, 0.8)
COUPLE = (0.08, 0.16, 0.24)
FAR_SCALE = 4.0
HALO = 2 * SUBSTEPS
PAD = 8
TILE = 16
MESH = pl.DeviceIdType.MESH


def split_host(array):
    high = array.astype(jnp.bfloat16)
    low = (array - high.astype(np.float64)).astype(jnp.bfloat16)
    return high, low


def split(value):
    high = value.astype(jnp.bfloat16)
    low = (value - high.astype(jnp.float32)).astype(jnp.bfloat16)
    return high, low


def dot(left, right, transposed=False):
    contract = ((1,), (1,)) if transposed else ((1,), (0,))
    return lax.dot_general(
        left, right, (contract, ((), ())), preferred_element_type=jnp.float32
    )


def dot3(left, right, transposed=False):
    return (
        dot(left[0], right[0], transposed)
        + dot(left[1], right[0], transposed)
        + dot(left[0], right[1], transposed)
    )


def sine_cosine(angle):
    square = angle * angle
    sine = 1.0
    for term in (11, 9, 7, 5, 3):
        sine = 1.0 - square * (1.0 / (term * (term - 1))) * sine
    cosine = 1.0
    for term in (12, 10, 8, 6, 4, 2):
        cosine = 1.0 - square * (1.0 / (term * (term - 1))) * cosine
    return angle * sine, cosine


def rates(window, turn):
    current, laplace, moving = [], [], []
    rows = TILE
    for channel in range(6):
        block = window[channel]
        whole = block.shape[0]
        width = block.shape[1]
        cur = block[8 : 8 + rows]
        left = pltpu.roll(block, 1, 0)[8 : 8 + rows]
        right = pltpu.roll(block, whole - 1, 0)[8 : 8 + rows]
        lane = lax.broadcasted_iota(jnp.int32, cur.shape, 1)
        above = jnp.where(lane == 0, 0.0, pltpu.roll(cur, 1, 1))
        below = jnp.where(lane == width - 1, 0.0, pltpu.roll(cur, width - 1, 1))
        drift = WALKOFF[channel // 2]
        current.append(cur)
        laplace.append(above + below + left + right - 4.0 * cur)
        if drift > 0:
            moving.append(-drift * (cur - left))
        else:
            moving.append(-drift * (right - cur))
    a1r, a1i, a2r, a2i, a3r, a3i = current
    pr = a1r * a2r - a1i * a2i
    pi = a1r * a2i + a1i * a2r
    if turn is None:
        br, bi = a3r, a3i
        m3r, m3i = pr, pi
    else:
        cosine, sine = turn
        br = a3r * cosine + a3i * sine
        bi = a3i * cosine - a3r * sine
        m3r = pr * cosine - pi * sine
        m3i = pi * cosine + pr * sine
    mixing = (
        (br * a2r + bi * a2i, bi * a2r - br * a2i),
        (br * a1r + bi * a1i, bi * a1r - br * a1i),
        (m3r, m3i),
    )
    result = []
    for wave in range(3):
        spread, strength = DIFFRACT[wave], COUPLE[wave]
        mr, mi = mixing[wave]
        result.append(moving[2 * wave] - spread * laplace[2 * wave + 1] - strength * mi)
        result.append(moving[2 * wave + 1] + spread * laplace[2 * wave] + strength * mr)
    return current, result


def kernel(
    devices,
    w1_ref,
    w2_ref,
    mis_ref,
    plate_ref,
    low_ref,
    high_ref,
    rgain_ref,
    cgain_ref,
    lhigh_hbm,
    llow_hbm,
    thigh_hbm,
    tlow_hbm,
    shigh_hbm,
    slow_hbm,
    third_ref,
    far_ref,
    back_ref,
    lhigh,
    llow,
    thigh,
    tlow,
    shigh,
    slow,
    fields,
    trial,
    turns,
    edge_out,
    edge_in,
    mis_wide,
    g_out,
    g_in,
    h_out,
    h_in,
    table_sem,
    edge_send,
    edge_recv,
    g_send,
    g_recv,
    h_send,
    h_recv,
):
    me = lax.axis_index("gx")
    row_count, width_here = mis_ref.shape
    far_rows = rgain_ref.shape[1]
    far_columns = cgain_ref.shape[1]
    block = far_rows // devices
    classes = far_columns // width_here
    scale = FAR_SCALE / math.sqrt(row_count * width_here * devices)
    wide = width_here + 2 * HALO
    tiles = wide // TILE

    def place(index):
        return (index - devices // 2 + classes // 2) % classes

    tables = [
        pltpu.make_async_copy(src, dst, table_sem.at[i])
        for i, (src, dst) in enumerate(
            (
                (lhigh_hbm, lhigh),
                (llow_hbm, llow),
                (shigh_hbm, shigh),
                (slow_hbm, slow),
                (thigh_hbm, thigh),
                (tlow_hbm, tlow),
            )
        )
    ]
    for copy in tables:
        copy.start()

    barrier = pltpu.get_barrier_semaphore()

    @pl.loop(1, devices)
    def _(k):
        pl.semaphore_signal(
            barrier, inc=1, device_id={"gx": lax.rem(me + k, devices)}, device_id_type=MESH
        )

    planes = [w1_ref[0], w1_ref[1], w2_ref[0], w2_ref[1], mis_ref[...]]
    own = PAD + HALO
    for plane, value in enumerate(planes):
        turned = value.T
        edge_out[0, plane * HALO : (plane + 1) * HALO, :] = turned[:HALO]
        edge_out[1, plane * HALO : (plane + 1) * HALO, :] = turned[width_here - HALO :]
        if plane < 4:
            fields[plane, own : own + width_here, :] = turned
        else:
            mis_wide[HALO : HALO + width_here, :] = turned
    for plane in (4, 5):
        fields[plane] = jnp.zeros(fields.shape[1:], jnp.float32)
    edge = jnp.zeros((PAD, row_count), jnp.float32)
    for plane in range(6):
        for start in (0, PAD + wide):
            fields[plane, start : start + PAD, :] = edge
            trial[plane, start : start + PAD, :] = edge

    pl.semaphore_wait(barrier, devices - 1)

    def edge_copy(side):
        return pltpu.make_async_remote_copy(
            src_ref=edge_out.at[side],
            dst_ref=edge_in.at[1 - side],
            send_sem=edge_send.at[side],
            recv_sem=edge_recv.at[1 - side],
            device_id={"gx": me - 1 if side == 0 else me + 1},
            device_id_type=MESH,
        )

    @pl.when(me > 0)
    def _():
        edge_copy(0).start()

    @pl.when(me < devices - 1)
    def _():
        edge_copy(1).start()

    @pl.when(me > 0)
    def _():
        edge_copy(1).wait_recv()

    @pl.when(me == 0)
    def _():
        edge_in[0] = jnp.zeros(edge_in.shape[1:], jnp.float32)

    @pl.when(me < devices - 1)
    def _():
        edge_copy(0).wait_recv()

    @pl.when(me == devices - 1)
    def _():
        edge_in[1] = jnp.zeros(edge_in.shape[1:], jnp.float32)

    for side, start in ((0, 0), (1, HALO + width_here)):
        for plane in range(5):
            value = edge_in[side, plane * HALO : (plane + 1) * HALO, :]
            if plane < 4:
                fields[plane, PAD + start : PAD + start + HALO, :] = value
            else:
                mis_wide[start : start + HALO, :] = value

    @pl.loop(0, tiles)
    def _(t):
        here = pl.ds(pl.multiple_of(t * TILE, TILE), TILE)
        sine, cosine = sine_cosine(mis_wide[here, :])
        c2 = cosine * cosine - sine * sine
        s2 = 2.0 * sine * cosine
        powers = (
            (cosine, sine),
            (c2, s2),
            (c2 * cosine - s2 * sine, s2 * cosine + c2 * sine),
            (c2 * c2 - s2 * s2, 2.0 * s2 * c2),
        )
        for z, (c, s) in enumerate(powers):
            turns[z, 0, here, :] = c
            turns[z, 1, here, :] = s

    lowest = jnp.where(me == 0, HALO, 0)
    highest = jnp.where(me == devices - 1, HALO + width_here, wide)

    def stage(source, position, finish):
        @pl.loop(0, tiles)
        def _(t):
            first = pl.multiple_of(t * TILE, 8)
            here = pl.ds(pl.multiple_of(first + PAD, 8), TILE)
            window = [source[c, pl.ds(first, TILE + 16), :] for c in range(6)]
            turn = None
            if position:
                at = pl.ds(first, TILE)
                turn = (turns[position - 1, 0, at, :], turns[position - 1, 1, at, :])
            current, rate = rates(window, turn)
            row = first + lax.broadcasted_iota(jnp.int32, current[0].shape, 0)
            inside = (row >= lowest) & (row < highest)
            for c in range(6):
                finish(c, here, current[c], rate[c], inside)

    for substep in range(SUBSTEPS):

        def predict(c, here, current, rate, inside):
            trial[c, here, :] = jnp.where(inside, current + rate, 0.0)

        def correct(c, here, current, rate, inside):
            value = 0.5 * (fields[c, here, :] + (current + rate))
            fields[c, here, :] = jnp.where(inside, value, 0.0)

        stage(fields, substep, predict)
        stage(trial, substep + 1, correct)

    step = 2.0 * math.pi / LEVELS
    plate_rows, plate_columns = plate_ref.shape

    def phases(shape, rows_first):
        sub = lax.broadcasted_iota(jnp.int32, shape, 0)
        lane = lax.broadcasted_iota(jnp.int32, shape, 1) // PLATE
        level = jnp.zeros(shape, jnp.int32)
        for r in range(plate_rows):
            for c in range(plate_columns):
                at = (sub == r) & (lane == c) if rows_first else (sub == c) & (lane == r)
                level = jnp.where(at, plate_ref[r, c], level)
        angle = step * level.astype(jnp.float32)
        return jnp.cos(angle), jnp.sin(angle)

    def spread(value, count):
        return jnp.concatenate(
            [
                jnp.broadcast_to(value[i : i + 1], (PLATE, value.shape[1]))
                for i in range(count)
            ],
            axis=0,
        )

    across = phases((max(8, plate_columns), row_count), False)
    cosine, sine = (spread(v, plate_columns) for v in across)
    tr = fields[4, own : own + width_here, :]
    ti = fields[5, own : own + width_here, :]
    nr = tr * cosine - ti * sine
    ni = tr * sine + ti * cosine
    near = split(
        jnp.concatenate(
            [
                jnp.concatenate([nr, ni], axis=1),
                jnp.concatenate([ni, -nr], axis=1),
            ],
            axis=0,
        )
    )
    tables[0].wait()
    tables[1].wait()
    chunks = max(1, far_rows // 128)
    chunk = far_rows // chunks
    per = chunk // block
    for n in range(chunks):
        at = slice(n * chunk, (n + 1) * chunk)
        g = dot3((lhigh[at, :], llow[at, :]), near, True)
        for j in range(per):
            rows = slice(j * block, (j + 1) * block)
            g_out[n * per + j, :block, :] = g[rows, :width_here]
            g_out[n * per + j, block:, :] = g[rows, width_here:]

    def g_copy(target, source):
        return pltpu.make_async_remote_copy(
            src_ref=g_out.at[target],
            dst_ref=g_in.at[source],
            send_sem=g_send.at[target],
            recv_sem=g_recv.at[source],
            device_id={"gx": target},
            device_id_type=MESH,
        )

    @pl.loop(1, devices)
    def _(k):
        g_copy(lax.rem(me + k, devices), me).start()

    g_in[me] = g_out[me]
    third_ref[0] = tr.T
    third_ref[1] = ti.T

    lane = lax.broadcasted_iota(jnp.int32, (block, far_rows), 1)
    row = me * block + lax.broadcasted_iota(jnp.int32, (block, far_rows), 0)

    def pick(ref):
        value = jnp.broadcast_to(ref[...].astype(jnp.float32), (block, far_rows))
        return jnp.sum(jnp.where(lane == row, value, 0.0), axis=1, keepdims=True)

    spot_low, spot_high, row_gain = pick(low_ref), pick(high_ref), pick(rgain_ref)
    gain = row_gain * cgain_ref[...]

    tables[2].wait()
    tables[3].wait()

    @pl.loop(1, devices)
    def _(k):
        source = lax.rem(me + k, devices)
        g_copy(source, source).wait_recv()

    folded = []
    for position in range(classes):
        total = None
        for source in range(devices):
            if place(source) == position:
                total = g_in[source] if total is None else total + g_in[source]
        folded.append(total)
    spectrum = dot3(split(jnp.concatenate(folded, axis=1)), (shigh[...], slow[...]))
    far_r = scale * (spectrum[:block, :far_columns] + spectrum[block:, far_columns:])
    far_i = scale * (spectrum[block:, :far_columns] - spectrum[:block, far_columns:])
    far_ref[0] = far_r
    far_ref[1] = far_i
    magnitude = jnp.sqrt(far_r * far_r + far_i * far_i)
    column = lax.broadcasted_iota(jnp.int32, far_r.shape, 1).astype(jnp.float32)
    inside = (column >= spot_low) & (column < spot_high)
    factor = jnp.where(inside, gain / jnp.maximum(magnitude, 1.0), 1.0)
    replaced = split(jnp.concatenate([far_r * factor, far_i * factor], axis=0))
    turned = dot3(replaced, (shigh[...], slow[...]))
    hr = turned[:block, :far_columns] - turned[block:, far_columns:]
    hi = turned[block:, :far_columns] + turned[:block, far_columns:]
    for position in range(classes):
        at = slice(position * width_here, (position + 1) * width_here)
        h_out[position, :block, :] = hr[:, at]
        h_out[position, block:, :] = hi[:, at]

    def h_copy(target, source):
        return pltpu.make_async_remote_copy(
            src_ref=h_out.at[place(target)],
            dst_ref=h_in.at[source],
            send_sem=h_send.at[target],
            recv_sem=h_recv.at[source],
            device_id={"gx": target},
            device_id_type=MESH,
        )

    @pl.loop(1, devices)
    def _(k):
        h_copy(lax.rem(me + k, devices), me).start()

    h_in[me] = h_out[place(me)]
    down = phases((max(8, plate_rows), width_here), True)
    cosine, sine = (spread(v, plate_rows) for v in down)
    tables[4].wait()
    tables[5].wait()

    @pl.loop(1, devices)
    def _(k):
        source = lax.rem(me + k, devices)
        h_copy(source, source).wait_recv()

    gathered = jnp.concatenate(
        [
            jnp.concatenate([h_in[s, :block, :], h_in[s, block:, :]], axis=1)
            for s in range(devices)
        ],
        axis=0,
    )
    summed = dot3((thigh[...], tlow[...]), split(gathered))
    br = scale * (summed[:row_count, :width_here] - summed[row_count:, width_here:])
    bi = scale * (summed[:row_count, width_here:] + summed[row_count:, :width_here])
    back_ref[0] = br * cosine + bi * sine
    back_ref[1] = bi * cosine - br * sine

    @pl.when(me > 0)
    def _():
        edge_copy(0).wait_send()

    @pl.when(me < devices - 1)
    def _():
        edge_copy(1).wait_send()

    @pl.loop(1, devices)
    def _(k):
        target = lax.rem(me + k, devices)
        g_copy(target, me).wait_send()
        h_copy(target, me).wait_send()


def local(wave_one, wave_two, mismatch, plate, spot_low, spot_high, row_gain, column_gain):
    devices = lax.axis_size("gx")
    row_count, width_here = mismatch.shape
    far_rows = row_gain.shape[0]
    far_columns = column_gain.shape[0]
    block = far_rows // devices
    classes = far_columns // width_here

    def angle_table(first, second, period):
        turns = np.mod(first[:, None] * second[None, :], period)
        angle = 2.0 * np.pi / period * turns
        return np.cos(angle), np.sin(angle)

    row_table = np.concatenate(
        angle_table(
            np.arange(far_rows) - far_rows // 2,
            np.arange(row_count) - row_count // 2,
            ZOOM * row_count,
        ),
        axis=1,
    )
    around = np.arange(far_columns) - far_columns // 2
    column_table = np.concatenate(angle_table(around, around, far_columns), axis=1)
    tables = (
        *split_host(row_table),
        *split_host(row_table.T),
        *split_host(column_table),
    )
    tables = [jnp.asarray(t) for t in tables]
    wide = width_here + 2 * HALO
    vmem = pl.BlockSpec(memory_space=pltpu.VMEM)
    smem = pl.BlockSpec(memory_space=pltpu.SMEM)
    anywhere = pl.BlockSpec(memory_space=pl.ANY)
    f32 = jnp.float32
    dma = pltpu.SemaphoreType.DMA

    def body(*refs):
        kernel(devices, *refs)

    return pl.pallas_call(
        body,
        out_shape=(
            jax.ShapeDtypeStruct((2, row_count, width_here), f32),
            jax.ShapeDtypeStruct((2, block, far_columns), f32),
            jax.ShapeDtypeStruct((2, row_count, width_here), f32),
        ),
        in_specs=[vmem] * 3 + [smem] + [vmem] * 4 + [anywhere] * 6,
        out_specs=(vmem,) * 3,
        scratch_shapes=[
            *[pltpu.VMEM(t.shape, t.dtype) for t in tables],
            pltpu.VMEM((6, wide + 2 * PAD, row_count), f32),
            pltpu.VMEM((6, wide + 2 * PAD, row_count), f32),
            pltpu.VMEM((SUBSTEPS, 2, wide, row_count), f32),
            pltpu.VMEM((2, 5 * HALO, row_count), f32),
            pltpu.VMEM((2, 5 * HALO, row_count), f32),
            pltpu.VMEM((wide, row_count), f32),
            pltpu.VMEM((devices, 2 * block, width_here), f32),
            pltpu.VMEM((devices, 2 * block, width_here), f32),
            pltpu.VMEM((classes, 2 * block, width_here), f32),
            pltpu.VMEM((devices, 2 * block, width_here), f32),
            dma((6,)),
            dma((2,)),
            dma((2,)),
            dma((devices,)),
            dma((devices,)),
            dma((devices,)),
            dma((devices,)),
        ],
        compiler_params=pltpu.CompilerParams(
            collective_id=0, has_side_effects=True, vmem_limit_bytes=48 * 1024 * 1024
        ),
    )(
        wave_one,
        wave_two,
        mismatch,
        plate,
        spot_low[None],
        spot_high[None],
        row_gain[None],
        column_gain[None],
        *tables,
    )


def solution(mesh):
    return jax.shard_map(
        local,
        mesh=mesh,
        in_specs=(
            P(None, "groups", "gx"),
            P(None, "groups", "gx"),
            P("groups", "gx"),
            P("groups", "gx"),
            P("groups"),
            P("groups"),
            P("groups"),
            P("groups"),
        ),
        out_specs=(
            P(None, "groups", "gx"),
            P(None, ("groups", "gx"), None),
            P(None, "groups", "gx"),
        ),
        check_vma=False,
    )
```

```python
import math

import jax
import jax.numpy as jnp
from jax import lax
from jax.experimental import pallas as pl
from jax.experimental.pallas import tpu as pltpu
from jax.sharding import PartitionSpec as P

SUBSTEPS = 4
ZOOM = 4
LEVELS = 16
PLATE = 32

DIFFRACT = (0.08, 0.04, 0.027)
WALKOFF = (0.3, -0.8, 0.8)
COUPLE = (0.08, 0.16, 0.24)
FAR_SCALE = 4.0
HALO = 2 * SUBSTEPS
PAD = 8
TILE = 16
MESH = pl.DeviceIdType.MESH


def split(value):
    high = value.astype(jnp.bfloat16)
    low = (value - high.astype(jnp.float32)).astype(jnp.bfloat16)
    return high, low


def dot(left, right, transposed=False):
    contract = ((1,), (1,)) if transposed else ((1,), (0,))
    return lax.dot_general(
        left, right, (contract, ((), ())), preferred_element_type=jnp.float32
    )


def dot3(left, right, transposed=False):
    return (
        dot(left[0], right[0], transposed)
        + dot(left[1], right[0], transposed)
        + dot(left[0], right[1], transposed)
    )


def sine_cosine(angle):
    square = angle * angle
    sine = 1.0
    for term in (11, 9, 7, 5, 3):
        sine = 1.0 - square * (1.0 / (term * (term - 1))) * sine
    cosine = 1.0
    for term in (12, 10, 8, 6, 4, 2):
        cosine = 1.0 - square * (1.0 / (term * (term - 1))) * cosine
    return angle * sine, cosine


def wave_table(high, low, rows, lanes, shifts, period, sine_at):
    shape = (TILE, lanes)
    lane = lax.broadcasted_iota(jnp.int32, shape, 1) - shifts[1]
    row = lax.broadcasted_iota(jnp.int32, shape, 0) - shifts[0]

    def turn(product):
        angle = (2.0 * math.pi / period) * (product & (period - 1)).astype(jnp.float32)
        return jnp.cos(angle), jnp.sin(angle)

    first = turn(row * lane)
    step = turn(TILE * lane[:8])
    step = [jnp.concatenate([v, v], axis=0) for v in step]

    def body(i, carry):
        at = pl.multiple_of(i * TILE, TILE)
        for value, (down, across) in zip(carry, ((0, 0), sine_at)):
            here = (pl.ds(pl.multiple_of(at + down, TILE), TILE), slice(across, across + lanes))
            high[here], low[here] = split(value)
        cosine, sine = carry
        return (
            cosine * step[0] - sine * step[1],
            sine * step[0] + cosine * step[1],
        )

    lax.fori_loop(0, rows // TILE, body, first)


def rates(window, turn, only_third):
    current, laplace, moving = [], [], []
    rows = TILE
    for channel in range(6):
        block = window[channel]
        if only_third and channel < 4:
            current.append(block[8 : 8 + rows])
            laplace.append(None)
            moving.append(None)
            continue
        whole = block.shape[0]
        width = block.shape[1]
        cur = block[8 : 8 + rows]
        left = pltpu.roll(block, 1, 0)[8 : 8 + rows]
        right = pltpu.roll(block, whole - 1, 0)[8 : 8 + rows]
        lane = lax.broadcasted_iota(jnp.int32, cur.shape, 1)
        above = jnp.where(lane == 0, 0.0, pltpu.roll(cur, 1, 1))
        below = jnp.where(lane == width - 1, 0.0, pltpu.roll(cur, width - 1, 1))
        drift = WALKOFF[channel // 2]
        current.append(cur)
        laplace.append(above + below + left + right - 4.0 * cur)
        if drift > 0:
            moving.append(-drift * (cur - left))
        else:
            moving.append(-drift * (right - cur))
    a1r, a1i, a2r, a2i, a3r, a3i = current
    pr = a1r * a2r - a1i * a2i
    pi = a1r * a2i + a1i * a2r
    if turn is None:
        br, bi = a3r, a3i
        m3r, m3i = pr, pi
    else:
        cosine, sine = turn
        br = a3r * cosine + a3i * sine
        bi = a3i * cosine - a3r * sine
        m3r = pr * cosine - pi * sine
        m3i = pi * cosine + pr * sine
    mixing = (
        (br * a2r + bi * a2i, bi * a2r - br * a2i),
        (br * a1r + bi * a1i, bi * a1r - br * a1i),
        (m3r, m3i),
    )
    result = []
    for wave in range(2 if only_third else 0, 3):
        spread, strength = DIFFRACT[wave], COUPLE[wave]
        mr, mi = mixing[wave]
        result.append(moving[2 * wave] - spread * laplace[2 * wave + 1] - strength * mi)
        result.append(moving[2 * wave + 1] + spread * laplace[2 * wave] + strength * mr)
    return current[4:] if only_third else current, result


def kernel(
    devices,
    w1_hbm,
    w2_hbm,
    mis_hbm,
    plate_hbm,
    low_hbm,
    high_hbm,
    rgain_hbm,
    cgain_hbm,
    third_ref,
    far_ref,
    back_ref,
    w1_ref,
    w2_ref,
    mis_ref,
    plate_ref,
    low_ref,
    high_ref,
    rgain_ref,
    cgain_ref,
    lhigh,
    llow,
    thigh,
    tlow,
    shigh,
    slow,
    fields,
    trial,
    turns,
    edge_out,
    edge_in,
    mis_wide,
    g_out,
    g_in,
    h_out,
    h_in,
    input_sem,
    edge_send,
    edge_recv,
    g_send,
    g_recv,
    h_send,
    h_recv,
):
    me = lax.axis_index("gx")
    row_count, width_here = mis_ref.shape
    far_rows = rgain_ref.shape[1]
    far_columns = cgain_ref.shape[1]
    block = far_rows // devices
    classes = far_columns // width_here
    scale = FAR_SCALE / math.sqrt(row_count * width_here * devices)
    wide = width_here + 2 * HALO
    tiles = wide // TILE

    def place(index):
        return (index - devices // 2 + classes // 2) % classes

    inputs = [
        pltpu.make_async_copy(src, dst, input_sem.at[i])
        for i, (src, dst) in enumerate(
            (
                (w1_hbm, w1_ref),
                (w2_hbm, w2_ref),
                (mis_hbm, mis_ref),
                (plate_hbm, plate_ref),
                (low_hbm, low_ref),
                (high_hbm, high_ref),
                (rgain_hbm, rgain_ref),
                (cgain_hbm, cgain_ref),
            )
        )
    ]
    for copy in inputs:
        copy.start()

    barrier = pltpu.get_barrier_semaphore()

    @pl.loop(1, devices)
    def _(k):
        pl.semaphore_signal(
            barrier, inc=1, device_id={"gx": lax.rem(me + k, devices)}, device_id_type=MESH
        )

    row_period = ZOOM * row_count
    half = (far_rows // 2, row_count // 2)
    wave_table(lhigh, llow, far_rows, row_count, half, row_period, (0, row_count))
    for copy in inputs:
        copy.wait()

    planes = [w1_ref[0], w1_ref[1], w2_ref[0], w2_ref[1], mis_ref[...]]
    own = PAD + HALO
    for plane, value in enumerate(planes):
        turned = value.T
        edge_out[0, plane * HALO : (plane + 1) * HALO, :] = turned[:HALO]
        edge_out[1, plane * HALO : (plane + 1) * HALO, :] = turned[width_here - HALO :]
        if plane < 4:
            fields[plane, own : own + width_here, :] = turned
        else:
            mis_wide[HALO : HALO + width_here, :] = turned
    for plane in (4, 5):
        fields[plane] = jnp.zeros(fields.shape[1:], jnp.float32)
    edge = jnp.zeros((PAD, row_count), jnp.float32)
    for plane in range(6):
        for start in (0, PAD + wide):
            fields[plane, start : start + PAD, :] = edge
            trial[plane, start : start + PAD, :] = edge

    pl.semaphore_wait(barrier, devices - 1)

    def edge_copy(side):
        return pltpu.make_async_remote_copy(
            src_ref=edge_out.at[side],
            dst_ref=edge_in.at[1 - side],
            send_sem=edge_send.at[side],
            recv_sem=edge_recv.at[1 - side],
            device_id={"gx": me - 1 if side == 0 else me + 1},
            device_id_type=MESH,
        )

    @pl.when(me > 0)
    def _():
        edge_copy(0).start()

    @pl.when(me < devices - 1)
    def _():
        edge_copy(1).start()

    wave_table(
        shigh, slow, far_columns, far_columns, (far_columns // 2,) * 2, far_columns,
        (0, far_columns),
    )
    wave_table(thigh, tlow, row_count, far_rows, half[::-1], row_period, (row_count, 0))

    @pl.when(me > 0)
    def _():
        edge_copy(1).wait_recv()

    @pl.when(me == 0)
    def _():
        edge_in[0] = jnp.zeros(edge_in.shape[1:], jnp.float32)

    @pl.when(me < devices - 1)
    def _():
        edge_copy(0).wait_recv()

    @pl.when(me == devices - 1)
    def _():
        edge_in[1] = jnp.zeros(edge_in.shape[1:], jnp.float32)

    for side, start in ((0, 0), (1, HALO + width_here)):
        for plane in range(5):
            value = edge_in[side, plane * HALO : (plane + 1) * HALO, :]
            if plane < 4:
                fields[plane, PAD + start : PAD + start + HALO, :] = value
            else:
                mis_wide[start : start + HALO, :] = value

    @pl.loop(0, tiles)
    def _(t):
        here = pl.ds(pl.multiple_of(t * TILE, TILE), TILE)
        sine, cosine = sine_cosine(mis_wide[here, :])
        c2 = cosine * cosine - sine * sine
        s2 = 2.0 * sine * cosine
        powers = (
            (cosine, sine),
            (c2, s2),
            (c2 * cosine - s2 * sine, s2 * cosine + c2 * sine),
            (c2 * c2 - s2 * s2, 2.0 * s2 * c2),
        )
        for z, (c, s) in enumerate(powers):
            turns[z, 0, here, :] = c
            turns[z, 1, here, :] = s

    lowest = jnp.where(me == 0, HALO, 0)
    highest = jnp.where(me == devices - 1, HALO + width_here, wide)

    def stage(source, position, finish, only_third=False):
        @pl.loop(0, tiles)
        def _(t):
            first = pl.multiple_of(t * TILE, 8)
            here = pl.ds(pl.multiple_of(first + PAD, 8), TILE)
            window = [source[c, pl.ds(first, TILE + 16), :] for c in range(6)]
            turn = None
            if position:
                at = pl.ds(first, TILE)
                turn = (turns[position - 1, 0, at, :], turns[position - 1, 1, at, :])
            current, rate = rates(window, turn, only_third)
            row = first + lax.broadcasted_iota(jnp.int32, current[0].shape, 0)
            inside = (row >= lowest) & (row < highest)
            for c, value, change in zip(range(6 - len(rate), 6), current, rate):
                finish(c, here, value, change, inside)

    for substep in range(SUBSTEPS):

        def predict(c, here, current, rate, inside):
            trial[c, here, :] = jnp.where(inside, current + rate, 0.0)

        def correct(c, here, current, rate, inside):
            value = 0.5 * (fields[c, here, :] + (current + rate))
            fields[c, here, :] = jnp.where(inside, value, 0.0)

        stage(fields, substep, predict)
        stage(trial, substep + 1, correct, substep == SUBSTEPS - 1)

    step = 2.0 * math.pi / LEVELS
    plate_columns, plate_rows = plate_ref.shape

    def phases(shape, rows_first):
        sub = lax.broadcasted_iota(jnp.int32, shape, 0)
        lane = lax.broadcasted_iota(jnp.int32, shape, 1) // PLATE
        level = jnp.zeros(shape, jnp.int32)
        for r in range(plate_rows):
            for c in range(plate_columns):
                at = (sub == r) & (lane == c) if rows_first else (sub == c) & (lane == r)
                level = jnp.where(at, plate_ref[c, r], level)
        angle = step * level.astype(jnp.float32)
        return jnp.cos(angle), jnp.sin(angle)

    def spread(value, count):
        return jnp.concatenate(
            [
                jnp.broadcast_to(value[i : i + 1], (PLATE, value.shape[1]))
                for i in range(count)
            ],
            axis=0,
        )

    across = phases((max(8, plate_columns), row_count), False)
    cosine, sine = (spread(v, plate_columns) for v in across)
    tr = fields[4, own : own + width_here, :]
    ti = fields[5, own : own + width_here, :]
    nr = tr * cosine - ti * sine
    ni = tr * sine + ti * cosine
    near = split(
        jnp.concatenate(
            [
                jnp.concatenate([nr, ni], axis=1),
                jnp.concatenate([ni, -nr], axis=1),
            ],
            axis=0,
        )
    )
    def g_copy(target, source):
        return pltpu.make_async_remote_copy(
            src_ref=g_out.at[target],
            dst_ref=g_in.at[source],
            send_sem=g_send.at[target],
            recv_sem=g_recv.at[source],
            device_id={"gx": target},
            device_id_type=MESH,
        )

    per = max(1, devices // 4)
    chunk = per * block
    for n in range(devices // per):
        group = lax.rem(me // per + devices // per // 2 + n, devices // per)
        at = pl.ds(pl.multiple_of(group * chunk, chunk), chunk)
        g = dot3((lhigh[at, :], llow[at, :]), near, True)
        for j in range(per):
            rows = slice(j * block, (j + 1) * block)
            target = group * per + j
            g_out[target, :block, :] = g[rows, :width_here]
            g_out[target, block:, :] = g[rows, width_here:]

        for j in range(per):
            target = group * per + j

            @pl.when(target != me)
            def _():
                g_copy(target, me).start()

    g_in[me] = g_out[me]
    third_ref[0] = tr.T
    third_ref[1] = ti.T

    lane = lax.broadcasted_iota(jnp.int32, (block, far_rows), 1)
    row = me * block + lax.broadcasted_iota(jnp.int32, (block, far_rows), 0)

    def pick(ref):
        value = jnp.broadcast_to(ref[...].astype(jnp.float32), (block, far_rows))
        return jnp.sum(jnp.where(lane == row, value, 0.0), axis=1, keepdims=True)

    spot_low, spot_high, row_gain = pick(low_ref), pick(high_ref), pick(rgain_ref)
    gain = row_gain * cgain_ref[...]


    @pl.loop(1, devices)
    def _(k):
        source = lax.rem(me + k, devices)
        g_copy(source, source).wait_recv()

    folded = []
    for position in range(classes):
        total = None
        for source in range(devices):
            if place(source) == position:
                total = g_in[source] if total is None else total + g_in[source]
        folded.append(total)
    spectrum = dot3(split(jnp.concatenate(folded, axis=1)), (shigh[...], slow[...]))
    far_r = scale * (spectrum[:block, :far_columns] + spectrum[block:, far_columns:])
    far_i = scale * (spectrum[block:, :far_columns] - spectrum[:block, far_columns:])
    far_ref[0] = far_r
    far_ref[1] = far_i
    magnitude = jnp.sqrt(far_r * far_r + far_i * far_i)
    column = lax.broadcasted_iota(jnp.int32, far_r.shape, 1).astype(jnp.float32)
    inside = (column >= spot_low) & (column < spot_high)
    factor = jnp.where(inside, gain / jnp.maximum(magnitude, 1.0), 1.0)
    replaced = split(jnp.concatenate([far_r * factor, far_i * factor], axis=0))
    turned = dot3(replaced, (shigh[...], slow[...]))
    hr = turned[:block, :far_columns] - turned[block:, far_columns:]
    hi = turned[block:, :far_columns] + turned[:block, far_columns:]
    for position in range(classes):
        at = slice(position * width_here, (position + 1) * width_here)
        h_out[position, :block, :] = hr[:, at]
        h_out[position, block:, :] = hi[:, at]

    def h_copy(target, source):
        return pltpu.make_async_remote_copy(
            src_ref=h_out.at[place(target)],
            dst_ref=h_in.at[source],
            send_sem=h_send.at[target],
            recv_sem=h_recv.at[source],
            device_id={"gx": target},
            device_id_type=MESH,
        )

    @pl.loop(1, devices)
    def _(k):
        h_copy(lax.rem(me + k, devices), me).start()

    h_in[me] = h_out[place(me)]
    down = phases((max(8, plate_rows), width_here), True)
    cosine, sine = (spread(v, plate_rows) for v in down)

    @pl.loop(1, devices)
    def _(k):
        source = lax.rem(me + k, devices)
        h_copy(source, source).wait_recv()

    gathered = jnp.concatenate(
        [
            jnp.concatenate([h_in[s, :block, :], h_in[s, block:, :]], axis=1)
            for s in range(devices)
        ],
        axis=0,
    )
    summed = dot3((thigh[...], tlow[...]), split(gathered))
    br = scale * (summed[:row_count, :width_here] - summed[row_count:, width_here:])
    bi = scale * (summed[:row_count, width_here:] + summed[row_count:, :width_here])
    back_ref[0] = br * cosine + bi * sine
    back_ref[1] = bi * cosine - br * sine

    @pl.when(me > 0)
    def _():
        edge_copy(0).wait_send()

    @pl.when(me < devices - 1)
    def _():
        edge_copy(1).wait_send()

    @pl.loop(1, devices)
    def _(k):
        target = lax.rem(me + k, devices)
        g_copy(target, me).wait_send()
        h_copy(target, me).wait_send()


def local(wave_one, wave_two, mismatch, plate, spot_low, spot_high, row_gain, column_gain):
    devices = lax.axis_size("gx")
    row_count, width_here = mismatch.shape
    far_rows = row_gain.shape[0]
    far_columns = column_gain.shape[0]
    block = far_rows // devices
    classes = far_columns // width_here

    wide = width_here + 2 * HALO
    vmem = pl.BlockSpec(memory_space=pltpu.VMEM)
    hbm = pl.BlockSpec(memory_space=pltpu.HBM)
    f32, bf16 = jnp.float32, jnp.bfloat16
    dma = pltpu.SemaphoreType.DMA

    def body(*refs):
        kernel(devices, *refs)

    return pl.pallas_call(
        body,
        out_shape=(
            jax.ShapeDtypeStruct((2, row_count, width_here), f32),
            jax.ShapeDtypeStruct((2, block, far_columns), f32),
            jax.ShapeDtypeStruct((2, row_count, width_here), f32),
        ),
        in_specs=[hbm] * 8,
        out_specs=(vmem,) * 3,
        scratch_shapes=[
            pltpu.VMEM((2, row_count, width_here), f32),
            pltpu.VMEM((2, row_count, width_here), f32),
            pltpu.VMEM((row_count, width_here), f32),
            pltpu.SMEM(plate.shape[::-1], jnp.int32),
            pltpu.VMEM((1, far_rows), jnp.int32),
            pltpu.VMEM((1, far_rows), jnp.int32),
            pltpu.VMEM((1, far_rows), f32),
            pltpu.VMEM((1, far_columns), f32),
            pltpu.VMEM((far_rows, 2 * row_count), bf16),
            pltpu.VMEM((far_rows, 2 * row_count), bf16),
            pltpu.VMEM((2 * row_count, far_rows), bf16),
            pltpu.VMEM((2 * row_count, far_rows), bf16),
            pltpu.VMEM((far_columns, 2 * far_columns), bf16),
            pltpu.VMEM((far_columns, 2 * far_columns), bf16),
            pltpu.VMEM((6, wide + 2 * PAD, row_count), f32),
            pltpu.VMEM((6, wide + 2 * PAD, row_count), f32),
            pltpu.VMEM((SUBSTEPS, 2, wide, row_count), f32),
            pltpu.VMEM((2, 5 * HALO, row_count), f32),
            pltpu.VMEM((2, 5 * HALO, row_count), f32),
            pltpu.VMEM((wide, row_count), f32),
            pltpu.VMEM((devices, 2 * block, width_here), f32),
            pltpu.VMEM((devices, 2 * block, width_here), f32),
            pltpu.VMEM((classes, 2 * block, width_here), f32),
            pltpu.VMEM((devices, 2 * block, width_here), f32),
            dma((8,)),
            dma((2,)),
            dma((2,)),
            dma((devices,)),
            dma((devices,)),
            dma((devices,)),
            dma((devices,)),
        ],
        compiler_params=pltpu.CompilerParams(
            collective_id=0, has_side_effects=True, vmem_limit_bytes=67043328
        ),
    )(
        wave_one,
        wave_two,
        mismatch,
        plate.T,
        spot_low[None],
        spot_high[None],
        row_gain[None],
        column_gain[None],
    )


def solution(mesh):
    return jax.shard_map(
        local,
        mesh=mesh,
        in_specs=(
            P(None, "groups", "gx"),
            P(None, "groups", "gx"),
            P("groups", "gx"),
            P("groups", "gx"),
            P("groups"),
            P("groups"),
            P("groups"),
            P("groups"),
        ),
        out_specs=(
            P(None, "groups", "gx"),
            P(None, ("groups", "gx"), None),
            P(None, "groups", "gx"),
        ),
        check_vma=False,
    )
```

```python
import math

import jax
import jax.numpy as jnp
from jax import lax
from jax.experimental import pallas as pl
from jax.experimental.pallas import tpu as pltpu
from jax.sharding import PartitionSpec as P

SUBSTEPS = 4
ZOOM = 4
LEVELS = 16
PLATE = 32

DIFFRACT = (0.08, 0.04, 0.027)
WALKOFF = (0.3, -0.8, 0.8)
COUPLE = (0.08, 0.16, 0.24)
FAR_SCALE = 4.0
HALO = 2 * SUBSTEPS
PAD = 8
TILE = 16
MESH = pl.DeviceIdType.MESH


def split(value):
    high = value.astype(jnp.bfloat16)
    low = (value - high.astype(jnp.float32)).astype(jnp.bfloat16)
    return high, low


def dot(left, right, transposed=False):
    contract = ((1,), (1,)) if transposed else ((1,), (0,))
    return lax.dot_general(
        left, right, (contract, ((), ())), preferred_element_type=jnp.float32
    )


def dot3(left, right, transposed=False):
    return (
        dot(left[0], right[0], transposed)
        + dot(left[1], right[0], transposed)
        + dot(left[0], right[1], transposed)
    )


def sine_cosine(angle):
    square = angle * angle
    sine = 1.0
    for term in (11, 9, 7, 5, 3):
        sine = 1.0 - square * (1.0 / (term * (term - 1))) * sine
    cosine = 1.0
    for term in (12, 10, 8, 6, 4, 2):
        cosine = 1.0 - square * (1.0 / (term * (term - 1))) * cosine
    return angle * sine, cosine


def wave_table(high, low, rows, lanes, shifts, period, sine_at):
    shape = (TILE, lanes)
    lane = lax.broadcasted_iota(jnp.int32, shape, 1) - shifts[1]
    row = lax.broadcasted_iota(jnp.int32, shape, 0) - shifts[0]

    def turn(product):
        angle = (2.0 * math.pi / period) * (product & (period - 1)).astype(jnp.float32)
        return jnp.cos(angle), jnp.sin(angle)

    first = turn(row * lane)
    step = turn(TILE * lane[:8])
    step = [jnp.concatenate([v, v], axis=0) for v in step]

    def body(i, carry):
        at = pl.multiple_of(i * TILE, TILE)
        for value, (down, across) in zip(carry, ((0, 0), sine_at)):
            here = (pl.ds(pl.multiple_of(at + down, TILE), TILE), slice(across, across + lanes))
            high[here], low[here] = split(value)
        cosine, sine = carry
        return (
            cosine * step[0] - sine * step[1],
            sine * step[0] + cosine * step[1],
        )

    lax.fori_loop(0, rows // TILE, body, first)


def rates(window, turn, only_third):
    current, laplace, moving = [], [], []
    rows = TILE
    for channel in range(6):
        block = window[channel]
        if only_third and channel < 4:
            current.append(block[8 : 8 + rows])
            laplace.append(None)
            moving.append(None)
            continue
        whole = block.shape[0]
        width = block.shape[1]
        cur = block[8 : 8 + rows]
        left = pltpu.roll(block, 1, 0)[8 : 8 + rows]
        right = pltpu.roll(block, whole - 1, 0)[8 : 8 + rows]
        lane = lax.broadcasted_iota(jnp.int32, cur.shape, 1)
        above = jnp.where(lane == 0, 0.0, pltpu.roll(cur, 1, 1))
        below = jnp.where(lane == width - 1, 0.0, pltpu.roll(cur, width - 1, 1))
        drift = WALKOFF[channel // 2]
        current.append(cur)
        laplace.append(above + below + left + right - 4.0 * cur)
        if drift > 0:
            moving.append(-drift * (cur - left))
        else:
            moving.append(-drift * (right - cur))
    a1r, a1i, a2r, a2i, a3r, a3i = current
    pr = a1r * a2r - a1i * a2i
    pi = a1r * a2i + a1i * a2r
    if turn is None:
        br, bi = a3r, a3i
        m3r, m3i = pr, pi
    else:
        cosine, sine = turn
        br = a3r * cosine + a3i * sine
        bi = a3i * cosine - a3r * sine
        m3r = pr * cosine - pi * sine
        m3i = pi * cosine + pr * sine
    mixing = (
        (br * a2r + bi * a2i, bi * a2r - br * a2i),
        (br * a1r + bi * a1i, bi * a1r - br * a1i),
        (m3r, m3i),
    )
    result = []
    for wave in range(2 if only_third else 0, 3):
        spread, strength = DIFFRACT[wave], COUPLE[wave]
        mr, mi = mixing[wave]
        result.append(moving[2 * wave] - spread * laplace[2 * wave + 1] - strength * mi)
        result.append(moving[2 * wave + 1] + spread * laplace[2 * wave] + strength * mr)
    return current[4:] if only_third else current, result


def kernel(
    devices,
    w1_hbm,
    w2_hbm,
    mis_hbm,
    plate_hbm,
    low_hbm,
    high_hbm,
    rgain_hbm,
    cgain_hbm,
    third_ref,
    far_ref,
    back_ref,
    w1_ref,
    w2_ref,
    mis_ref,
    plate_ref,
    low_ref,
    high_ref,
    rgain_ref,
    cgain_ref,
    lhigh,
    llow,
    thigh,
    tlow,
    shigh,
    slow,
    fields,
    trial,
    turns,
    edge_out,
    edge_in,
    mis_wide,
    g_out,
    g_in,
    h_out,
    h_in,
    input_sem,
    edge_send,
    edge_recv,
    g_send,
    g_recv,
    h_send,
    h_recv,
):
    me = lax.axis_index("gx")
    row_count, width_here = mis_ref.shape
    far_rows = rgain_ref.shape[1]
    far_columns = cgain_ref.shape[1]
    block = far_rows // devices
    classes = far_columns // width_here
    scale = FAR_SCALE / math.sqrt(row_count * width_here * devices)
    wide = width_here + 2 * HALO
    half_width = width_here // 2
    half_rows = half_width + 2 * HALO

    def place(index):
        return (index - devices // 2 + classes // 2) % classes

    inputs = [
        pltpu.make_async_copy(src, dst, input_sem.at[i])
        for i, (src, dst) in enumerate(
            (
                (w1_hbm, w1_ref),
                (w2_hbm, w2_ref),
                (mis_hbm, mis_ref),
                (plate_hbm, plate_ref),
                (low_hbm, low_ref),
                (high_hbm, high_ref),
                (rgain_hbm, rgain_ref),
                (cgain_hbm, cgain_ref),
            )
        )
    ]
    for copy in inputs:
        copy.start()

    barrier = pltpu.get_barrier_semaphore()

    @pl.loop(1, devices)
    def _(k):
        pl.semaphore_signal(
            barrier, inc=1, device_id={"gx": lax.rem(me + k, devices)}, device_id_type=MESH
        )

    row_period = ZOOM * row_count
    middle = (far_rows // 2, row_count // 2)
    wave_table(lhigh, llow, far_rows, row_count, middle, row_period, (0, row_count))
    for copy in inputs:
        copy.wait()

    planes = [w1_ref[0], w1_ref[1], w2_ref[0], w2_ref[1], mis_ref[...]]
    own = PAD + HALO
    kept = half_width + HALO
    for plane, value in enumerate(planes):
        turned = value.T
        edge_out[0, plane * HALO : (plane + 1) * HALO, :] = turned[:HALO]
        edge_out[1, plane * HALO : (plane + 1) * HALO, :] = turned[width_here - HALO :]
        if plane < 4:
            fields[0, plane, own : own + kept, :] = turned[:kept]
            fields[1, plane, PAD : PAD + kept, :] = turned[width_here - kept :]
        else:
            mis_wide[HALO : HALO + width_here, :] = turned
    edge = jnp.zeros((PAD, row_count), jnp.float32)
    for plane in range(6):
        for start in (0, PAD + half_rows):
            trial[plane, start : start + PAD, :] = edge
            for h in range(2):
                fields[h, plane, start : start + PAD, :] = edge
    for h in range(2):
        for plane in (4, 5):
            fields[h, plane, PAD : PAD + half_rows, :] = jnp.zeros(
                (half_rows, row_count), jnp.float32
            )

    pl.semaphore_wait(barrier, devices - 1)

    def edge_copy(side):
        return pltpu.make_async_remote_copy(
            src_ref=edge_out.at[side],
            dst_ref=edge_in.at[1 - side],
            send_sem=edge_send.at[side],
            recv_sem=edge_recv.at[1 - side],
            device_id={"gx": me - 1 if side == 0 else me + 1},
            device_id_type=MESH,
        )

    @pl.when(me > 0)
    def _():
        edge_copy(0).start()

    @pl.when(me < devices - 1)
    def _():
        edge_copy(1).start()

    wave_table(
        shigh, slow, far_columns, far_columns, (far_columns // 2,) * 2, far_columns,
        (0, far_columns),
    )
    wave_table(thigh, tlow, row_count, far_rows, middle[::-1], row_period, (row_count, 0))

    def take_edge(side):
        there = me > 0 if side == 0 else me < devices - 1

        @pl.when(there)
        def _():
            edge_copy(1 - side).wait_recv()

        @pl.when(jnp.logical_not(there))
        def _():
            edge_in[side] = jnp.zeros(edge_in.shape[1:], jnp.float32)

        start = 0 if side == 0 else HALO + width_here
        at = PAD + start - side * half_width
        for plane in range(5):
            value = edge_in[side, plane * HALO : (plane + 1) * HALO, :]
            if plane < 4:
                fields[side, plane, at : at + HALO, :] = value
            else:
                mis_wide[start : start + HALO, :] = value

        start = side * half_rows
        count = half_rows if side == 0 else wide - half_rows

        @pl.loop(start // TILE, (start + count) // TILE)
        def _(t):
            here = pl.ds(pl.multiple_of(t * TILE, TILE), TILE)
            sine, cosine = sine_cosine(mis_wide[here, :])
            c2 = cosine * cosine - sine * sine
            s2 = 2.0 * sine * cosine
            powers = (
                (cosine, sine),
                (c2, s2),
                (c2 * cosine - s2 * sine, s2 * cosine + c2 * sine),
                (c2 * c2 - s2 * s2, 2.0 * s2 * c2),
            )
            for z, (c, s) in enumerate(powers):
                turns[z, 0, here, :] = c
                turns[z, 1, here, :] = s

    lowest = jnp.where(me == 0, HALO, 0)
    highest = jnp.where(me == devices - 1, HALO + width_here, wide)

    def stage(source, shift, position, finish, only_third=False):
        @pl.loop(0, half_rows // TILE)
        def _(t):
            first = pl.multiple_of(t * TILE, 8)
            here = pl.ds(pl.multiple_of(first + PAD, 8), TILE)
            window = [source[c, pl.ds(first, TILE + 16), :] for c in range(6)]
            turn = None
            if position:
                at = pl.ds(pl.multiple_of(first + shift, 8), TILE)
                turn = (turns[position - 1, 0, at, :], turns[position - 1, 1, at, :])
            current, rate = rates(window, turn, only_third)
            row = first + shift + lax.broadcasted_iota(jnp.int32, current[0].shape, 0)
            inside = (row >= lowest) & (row < highest)
            for c, value, change in zip(range(6 - len(rate), 6), current, rate):
                finish(c, here, value, change, inside)

    def crystal(h):
        for substep in range(SUBSTEPS):

            def predict(c, here, current, rate, inside):
                trial[c, here, :] = jnp.where(inside, current + rate, 0.0)

            def correct(c, here, current, rate, inside):
                value = 0.5 * (fields[h, c, here, :] + (current + rate))
                fields[h, c, here, :] = jnp.where(inside, value, 0.0)

            shift = h * half_width
            stage(fields.at[h], shift, substep, predict)
            stage(trial, shift, substep + 1, correct, substep == SUBSTEPS - 1)

    step = 2.0 * math.pi / LEVELS
    plate_columns, plate_rows = plate_ref.shape

    def phases(shape, rows_first):
        sub = lax.broadcasted_iota(jnp.int32, shape, 0)
        lane = lax.broadcasted_iota(jnp.int32, shape, 1) // PLATE
        level = jnp.zeros(shape, jnp.int32)
        for r in range(plate_rows):
            for c in range(plate_columns):
                at = (sub == r) & (lane == c) if rows_first else (sub == c) & (lane == r)
                level = jnp.where(at, plate_ref[c, r], level)
        angle = step * level.astype(jnp.float32)
        return jnp.cos(angle), jnp.sin(angle)

    def spread(value, count):
        return jnp.concatenate(
            [
                jnp.broadcast_to(value[i : i + 1], (PLATE, value.shape[1]))
                for i in range(count)
            ],
            axis=0,
        )

    across = phases((max(8, plate_columns), row_count), False)
    cosine, sine = (spread(v, plate_columns) for v in across)
    def g_copy(h, target, source):
        return pltpu.make_async_remote_copy(
            src_ref=g_out.at[h, target],
            dst_ref=g_in.at[h, source],
            send_sem=g_send.at[h, target],
            recv_sem=g_recv.at[h, source],
            device_id={"gx": target},
            device_id_type=MESH,
        )

    per = max(1, devices // 4)
    chunk = per * block
    for h in range(2):
        take_edge(h)
        crystal(h)
        tr = fields[h, 4, own : own + half_width, :]
        ti = fields[h, 5, own : own + half_width, :]
        turn = [v[h * half_width : (h + 1) * half_width] for v in (cosine, sine)]
        nr = tr * turn[0] - ti * turn[1]
        ni = tr * turn[1] + ti * turn[0]
        near = split(
            jnp.concatenate(
                [
                    jnp.concatenate([nr, ni], axis=1),
                    jnp.concatenate([ni, -nr], axis=1),
                ],
                axis=0,
            )
        )
        for n in range(devices // per):
            group = lax.rem(me // per + devices // per // 2 + n, devices // per)
            at = pl.ds(pl.multiple_of(group * chunk, chunk), chunk)
            g = dot3((lhigh[at, :], llow[at, :]), near, True)
            for j in range(per):
                g_out[h, group * per + j] = g[j * block : (j + 1) * block]

            for j in range(per):
                target = group * per + j

                @pl.when(target != me)
                def _():
                    g_copy(h, target, me).start()

        g_in[h, me] = g_out[h, me]

    for part in range(2):
        ends = [fields[h, 4 + part, own : own + half_width, :] for h in range(2)]
        third_ref[part] = jnp.concatenate(ends, axis=0).T

    lane = lax.broadcasted_iota(jnp.int32, (block, far_rows), 1)
    row = me * block + lax.broadcasted_iota(jnp.int32, (block, far_rows), 0)

    def pick(ref):
        value = jnp.broadcast_to(ref[...].astype(jnp.float32), (block, far_rows))
        return jnp.sum(jnp.where(lane == row, value, 0.0), axis=1, keepdims=True)

    spot_low, spot_high, row_gain = pick(low_ref), pick(high_ref), pick(rgain_ref)
    gain = row_gain * cgain_ref[...]


    @pl.loop(1, devices)
    def _(k):
        source = lax.rem(me + k, devices)
        g_copy(0, source, source).wait_recv()
        g_copy(1, source, source).wait_recv()

    real, imaginary = [], []
    for position in range(classes):
        for h in range(2):
            total = None
            for source in range(devices):
                if place(source) == position:
                    total = g_in[h, source] if total is None else total + g_in[h, source]
            real.append(total[:, :half_width])
            imaginary.append(total[:, half_width:])
    folded = jnp.concatenate(
        [jnp.concatenate(real, axis=1), jnp.concatenate(imaginary, axis=1)], axis=0
    )
    spectrum = dot3(split(folded), (shigh[...], slow[...]))
    far_r = scale * (spectrum[:block, :far_columns] + spectrum[block:, far_columns:])
    far_i = scale * (spectrum[block:, :far_columns] - spectrum[:block, far_columns:])
    far_ref[0] = far_r
    far_ref[1] = far_i
    magnitude = jnp.sqrt(far_r * far_r + far_i * far_i)
    column = lax.broadcasted_iota(jnp.int32, far_r.shape, 1).astype(jnp.float32)
    inside = (column >= spot_low) & (column < spot_high)
    factor = jnp.where(inside, gain / jnp.maximum(magnitude, 1.0), 1.0)
    replaced = split(jnp.concatenate([far_r * factor, far_i * factor], axis=0))
    turned = dot3(replaced, (shigh[...], slow[...]))
    hr = turned[:block, :far_columns] - turned[block:, far_columns:]
    hi = turned[block:, :far_columns] + turned[:block, far_columns:]
    for position in range(classes):
        at = slice(position * width_here, (position + 1) * width_here)
        h_out[position, :block, :] = hr[:, at]
        h_out[position, block:, :] = hi[:, at]

    def h_copy(target, source):
        return pltpu.make_async_remote_copy(
            src_ref=h_out.at[place(target)],
            dst_ref=h_in.at[source],
            send_sem=h_send.at[target],
            recv_sem=h_recv.at[source],
            device_id={"gx": target},
            device_id_type=MESH,
        )

    @pl.loop(1, devices)
    def _(k):
        h_copy(lax.rem(me + k, devices), me).start()

    h_in[me] = h_out[place(me)]
    down = phases((max(8, plate_rows), width_here), True)
    cosine, sine = (spread(v, plate_rows) for v in down)

    count = devices // 2
    summed = None
    for n in range(2):
        group = lax.rem(me // count + n, 2)

        @pl.loop(0, count)
        def _(k):
            source = group * count + k

            @pl.when(source != me)
            def _():
                h_copy(source, source).wait_recv()

        gathered = []
        for k in range(count):
            value = h_in[group * count + k]
            gathered.append(jnp.concatenate([value[:block], value[block:]], axis=1))
        at = pl.ds(pl.multiple_of(group * count * block, count * block), count * block)
        part = dot3(
            (thigh[:, at], tlow[:, at]), split(jnp.concatenate(gathered, axis=0))
        )
        summed = part if summed is None else summed + part
    br = scale * (summed[:row_count, :width_here] - summed[row_count:, width_here:])
    bi = scale * (summed[:row_count, width_here:] + summed[row_count:, :width_here])
    back_ref[0] = br * cosine + bi * sine
    back_ref[1] = bi * cosine - br * sine

    @pl.when(me > 0)
    def _():
        edge_copy(0).wait_send()

    @pl.when(me < devices - 1)
    def _():
        edge_copy(1).wait_send()

    @pl.loop(1, devices)
    def _(k):
        target = lax.rem(me + k, devices)
        g_copy(0, target, me).wait_send()
        g_copy(1, target, me).wait_send()
        h_copy(target, me).wait_send()


def local(wave_one, wave_two, mismatch, plate, spot_low, spot_high, row_gain, column_gain):
    devices = lax.axis_size("gx")
    row_count, width_here = mismatch.shape
    far_rows = row_gain.shape[0]
    far_columns = column_gain.shape[0]
    block = far_rows // devices
    classes = far_columns // width_here

    wide = width_here + 2 * HALO
    half_rows = width_here // 2 + 2 * HALO
    vmem = pl.BlockSpec(memory_space=pltpu.VMEM)
    hbm = pl.BlockSpec(memory_space=pltpu.HBM)
    f32, bf16 = jnp.float32, jnp.bfloat16
    dma = pltpu.SemaphoreType.DMA

    def body(*refs):
        kernel(devices, *refs)

    return pl.pallas_call(
        body,
        out_shape=(
            jax.ShapeDtypeStruct((2, row_count, width_here), f32),
            jax.ShapeDtypeStruct((2, block, far_columns), f32),
            jax.ShapeDtypeStruct((2, row_count, width_here), f32),
        ),
        in_specs=[hbm] * 8,
        out_specs=(vmem,) * 3,
        scratch_shapes=[
            pltpu.VMEM((2, row_count, width_here), f32),
            pltpu.VMEM((2, row_count, width_here), f32),
            pltpu.VMEM((row_count, width_here), f32),
            pltpu.SMEM(plate.shape[::-1], jnp.int32),
            pltpu.VMEM((1, far_rows), jnp.int32),
            pltpu.VMEM((1, far_rows), jnp.int32),
            pltpu.VMEM((1, far_rows), f32),
            pltpu.VMEM((1, far_columns), f32),
            pltpu.VMEM((far_rows, 2 * row_count), bf16),
            pltpu.VMEM((far_rows, 2 * row_count), bf16),
            pltpu.VMEM((2 * row_count, far_rows), bf16),
            pltpu.VMEM((2 * row_count, far_rows), bf16),
            pltpu.VMEM((far_columns, 2 * far_columns), bf16),
            pltpu.VMEM((far_columns, 2 * far_columns), bf16),
            pltpu.VMEM((2, 6, half_rows + 2 * PAD, row_count), f32),
            pltpu.VMEM((6, half_rows + 2 * PAD, row_count), f32),
            pltpu.VMEM((SUBSTEPS, 2, wide, row_count), f32),
            pltpu.VMEM((2, 5 * HALO, row_count), f32),
            pltpu.VMEM((2, 5 * HALO, row_count), f32),
            pltpu.VMEM((wide, row_count), f32),
            pltpu.VMEM((2, devices, block, width_here), f32),
            pltpu.VMEM((2, devices, block, width_here), f32),
            pltpu.VMEM((classes, 2 * block, width_here), f32),
            pltpu.VMEM((devices, 2 * block, width_here), f32),
            dma((8,)),
            dma((2,)),
            dma((2,)),
            dma((2, devices)),
            dma((2, devices)),
            dma((devices,)),
            dma((devices,)),
        ],
        compiler_params=pltpu.CompilerParams(
            collective_id=0, has_side_effects=True, vmem_limit_bytes=67043328
        ),
    )(
        wave_one,
        wave_two,
        mismatch,
        plate.T,
        spot_low[None],
        spot_high[None],
        row_gain[None],
        column_gain[None],
    )


def solution(mesh):
    return jax.shard_map(
        local,
        mesh=mesh,
        in_specs=(
            P(None, "groups", "gx"),
            P(None, "groups", "gx"),
            P("groups", "gx"),
            P("groups", "gx"),
            P("groups"),
            P("groups"),
            P("groups"),
            P("groups"),
        ),
        out_specs=(
            P(None, "groups", "gx"),
            P(None, ("groups", "gx"), None),
            P(None, "groups", "gx"),
        ),
        check_vma=False,
    )
```
